32 devices in a mesh: tm: 2 (over y), rows: 16 (over z, x, core).
Axes of the slice: x: 2, y: 2, z: 4, core: 2. Of those that a mesh axis runs over, the one named last changes fastest.
Arguments:
- frames_in: bfloat16 [8, 32, 96, 832], P('tm', 'rows'), may hold values from -6 to 6
- gain_first: float32 [96], replicated, may hold values from 0.1 to 1.9
- kernel_first: bfloat16 [3, 3, 3, 96, 96], replicated, may hold values from -0.125 to 0.125
- bias_first: float32 [96], replicated, may hold values from -3 to 3
- gain_second: float32 [96], replicated, may hold values from 0.1 to 1.9
- kernel_second: bfloat16 [3, 3, 3, 96, 96], replicated, may hold values from -0.125 to 0.125
- bias_second: float32 [96], replicated, may hold values from -3 to 3
Outputs:
- frames_out: bfloat16 [8, 32, 96, 832], P('tm', 'rows')
The draws below stay inside these ranges and needn't reach their ends.
All inputs are finite; a program needn't handle non-finite values.
Results may differ from the reference program's by a relative error of at most 0.008.
Values may be sent and summed in bfloat16 or wider, within the bound.
A program may use at most 128 MiB of HBM per device.

```python
import jax
import jax.numpy as jnp
from jax import lax

C = 96
W = 832
FRAMES = 8
H = 32


def block_levels(own_key, extent, cuts, smallest, top_value):
    level = 1.0
    for position, parts in cuts:
        heights = jax.random.uniform(jax.random.fold_in(jax.random.fold_in(own_key, 6), position), (parts,), jnp.float32, smallest / len(cuts), top_value / len(cuts))
        level = level * jnp.repeat(jnp.exp(heights), extent[position] // parts).reshape((-1,) + (1,) * (len(extent) - 1 - position))
    return level


def scatter_about(rng, dims, scale, limit, split=(), held_as=jnp.bfloat16):
    values = jax.random.normal(rng, dims, jnp.float32) * scale
    if len(split) > 0:
        values = block_levels(rng, dims, split, -0.22, 0.18) * values
    return jnp.clip(values, min=-limit, max=limit).astype(held_as)


def setup_inputs(seed: int = 0) -> dict:
    key_list = jax.random.split(jax.random.key(seed), 8)
    frames_in = scatter_about(key_list[0], (FRAMES, H, C, W), 1.0, 6.0, ((0, 2), (1, 16)))
    gain_first = jnp.clip(1.0 + 0.18 * jax.random.normal(key_list[1], (C,), jnp.float32), 0.1, 1.9)
    kernel_first = scatter_about(key_list[2], (3, 3, 3, C, C), (27 * C) ** -0.5, 0.125)
    bias_first = scatter_about(key_list[3], (C,), 0.5, 3.0, (), jnp.float32)
    gain_second = jnp.clip(1.0 + 0.18 * jax.random.normal(key_list[4], (C,), jnp.float32), 0.1, 1.9)
    kernel_second = scatter_about(key_list[5], (3, 3, 3, C, C), (27 * C) ** -0.5, 0.125)
    bias_second = scatter_about(key_list[6], (C,), 0.5, 3.0, (), jnp.float32)
    return {"frames_in": frames_in, "gain_first": gain_first, "kernel_first": kernel_first, "bias_first": bias_first, "gain_second": gain_second, "kernel_second": kernel_second, "bias_second": bias_second}


def norm_silu(values, gain):
    wide = values.astype(jnp.float32)
    mean_square = lax.optimization_barrier(jnp.mean(wide * wide, axis=-2, keepdims=True))
    scaled = wide * lax.rsqrt(mean_square + 1e-06) * gain[:, None]
    return jax.nn.silu(scaled).astype(jnp.bfloat16)

def conv_full(active, kernel, bias):
    count_t, count_h, channels, count_w = active.shape
    padded = jnp.pad(active, ((2, 0), (1, 1), (0, 0), (1, 1)))
    kernel_wide = kernel.astype(jnp.float32)

    def one_frame(index):
        window_slab = lax.dynamic_slice_in_dim(padded, index, 3, 0).astype(jnp.float32)
        total = jnp.zeros((count_h, channels, count_w), jnp.float32)
        for tap_t in range(3):
            for tap_r in range(3):
                for tap_w in range(3):
                    piece = window_slab[tap_t, tap_r:tap_r + count_h, :, tap_w:tap_w + count_w]
                    total = total + jnp.einsum('oc,hcw->how', kernel_wide[tap_t, tap_r, tap_w], piece)
        return total + bias[:, None]
    return lax.map(one_frame, jnp.arange(count_t, dtype=jnp.int32))

def reference(frames_in, gain_first, kernel_first, bias_first, gain_second, kernel_second, bias_second):
    act_first = norm_silu(frames_in, gain_first)
    hidden = conv_full(act_first, kernel_first, bias_first).astype(jnp.bfloat16)
    act_second = norm_silu(hidden, gain_second)
    result = conv_full(act_second, kernel_second, bias_second) + frames_in.astype(jnp.float32)
    return result.astype(jnp.bfloat16)
```

```python
import functools

import jax
import jax.numpy as jnp
from jax import lax
from jax.experimental import pallas as pl
from jax.experimental.pallas import tpu as pltpu
from jax.sharding import PartitionSpec as P


def norm_silu(values, gain):
    wide = values.astype(jnp.float32)
    mean_square = jnp.mean(wide * wide, axis=-2, keepdims=True)
    half = wide * lax.rsqrt(mean_square + 1e-06) * (0.5 * gain)
    return (half + half * jnp.tanh(half)).astype(jnp.bfloat16)


def shifted(block, axis, distance):
    devices = range(lax.axis_size(axis))
    route = [(i - distance, i) for i in devices if i - distance in devices]
    return lax.ppermute(block, axis, route)


def row_halo(block):
    return shifted(block[:, -1:], "rows", 1), shifted(block[:, :1], "rows", -1)


def act_kernel(frames, gain, out):
    for row in range(frames.shape[1]):
        out[0, row] = norm_silu(frames[0, row], gain[...])


def activate(frames, gain):
    count, rows, channels, pixels = frames.shape
    block = pl.BlockSpec((1, rows, channels, pixels), lambda i: (i, 0, 0, 0))
    return pl.pallas_call(
        act_kernel,
        grid=(count,),
        in_specs=[block, pl.BlockSpec((channels, 1), lambda i: (0, 0))],
        out_specs=block,
        out_shape=jax.ShapeDtypeStruct(frames.shape, jnp.bfloat16),
        name="activate",
    )(frames, gain)


def conv_kernel(groups, final, *refs):
    inputs, out = list(refs[:-1]), refs[-1]
    slabs = []
    for _ in range(groups):
        own, up, down = inputs[0], inputs[1], inputs[2]
        inputs = inputs[3:]
        for t in range(own.shape[0]):
            rows = [own.at[t, r] for r in range(own.shape[1])]
            slabs.append([up.at[t, 0]] + rows + [down.at[t, 0]])
    weight, bias, extra = inputs[0], inputs[1], inputs[2]
    frames, rows, channels, pixels = out.shape
    zero = jnp.zeros((channels, 1), jnp.float32)
    for t in range(frames):
        for r in range(rows):
            taps = [slabs[t + i][r + j][...] for i in range(3) for j in range(3)]
            sums = jnp.dot(
                weight[...], jnp.concatenate(taps, axis=0), preferred_element_type=jnp.float32
            )
            left = sums[:channels]
            right = sums[2 * channels :]
            result = (
                sums[channels : 2 * channels]
                + jnp.concatenate([zero, left[:, : pixels - 1]], axis=1)
                + jnp.concatenate([right[:, 1:], zero], axis=1)
                + bias[...]
            )
            if final:
                out[t, r] = (result + extra[t, r].astype(jnp.float32)).astype(jnp.bfloat16)
            else:
                out[t, r] = norm_silu(result.astype(jnp.bfloat16), extra[...])


def convolve(groups, weight, bias, extra, final, start=0, total=None, into=None, name="conv"):
    rows, channels, pixels = groups[0][0].shape[1:]
    count = sum(g[4] for g in groups) - 2
    operands, specs = [], []

    def whole(value):
        operands.append(value)
        specs.append(pl.BlockSpec(value.shape, lambda i, n=value.ndim: (0,) * n))

    for own, up, down, first, frames in groups:
        for value in (own, up, down):
            operands.append(value)
            specs.append(
                pl.BlockSpec((frames,) + value.shape[1:], lambda i, b=first // frames: (b, 0, 0, 0))
            )
    whole(weight)
    whole(bias)
    if final:
        operands.append(extra)
        specs.append(
            pl.BlockSpec((count, rows, channels, pixels), lambda i: (start // count, 0, 0, 0))
        )
    else:
        whole(extra)
    body = functools.partial(conv_kernel, len(groups), final)
    aliases = {}
    if into is not None:
        aliases = {len(operands): 0}
        operands.append(into)
        specs.append(pl.BlockSpec(memory_space=pl.ANY))
        plain = body

        def body(*refs):
            plain(*refs[:-2], refs[-1])

    return pl.pallas_call(
        body,
        grid=(1,),
        in_specs=specs,
        out_specs=pl.BlockSpec(
            (count, rows, channels, pixels), lambda i: (start // count, 0, 0, 0)
        ),
        out_shape=jax.ShapeDtypeStruct((total or count, rows, channels, pixels), jnp.bfloat16),
        input_output_aliases=aliases,
        compiler_params=pltpu.CompilerParams(vmem_limit_bytes=48 << 20),
        cost_estimate=pl.CostEstimate(
            flops=2 * 27 * channels * channels * pixels * rows * count * 2,
            bytes_accessed=8 << 20,
            transcendentals=0,
        ),
        name=name,
    )(*operands)


def on_device(
    frames_in, gain_first, kernel_first, bias_first, gain_second, kernel_second, bias_second
):
    frames, channels = frames_in.shape[0], frames_in.shape[2]
    half = frames // 2

    def matrix(kernel):
        return kernel.transpose(2, 3, 0, 1, 4).reshape(3 * channels, 9 * channels)

    first, second = matrix(kernel_first), matrix(kernel_second)
    bias_first, bias_second = bias_first[:, None], bias_second[:, None]
    gain_first, gain_second = gain_first[:, None], gain_second[:, None]

    act = activate(frames_in, gain_first)
    earlier = shifted(act[half:], "tm", 1)
    up, down = row_halo(act)
    late = convolve([(act, up, down, 0, frames)], first, bias_first, gain_second, False, name="late_first")
    earlier_up, earlier_down = row_halo(earlier)
    earlier_second = shifted(late, "tm", 1)
    late_up, late_down = row_halo(late)
    soon = convolve(
        [(earlier, earlier_up, earlier_down, 0, half), (act, up, down, 0, half)],
        first, bias_first, gain_second, False, name="soon_first",
    )
    soon_up, soon_down = row_halo(soon)
    second_up, second_down = row_halo(earlier_second)
    out = convolve(
        [(soon, soon_up, soon_down, 0, half), (late, late_up, late_down, 0, half)],
        second, bias_second, frames_in, True, half, frames, name="late_second",
    )
    return convolve(
        [(earlier_second, second_up, second_down, 0, half), (soon, soon_up, soon_down, 0, half)],
        second, bias_second, frames_in, True, 0, frames, into=out, name="soon_second",
    )


def solution(mesh):
    return jax.shard_map(
        on_device,
        mesh=mesh,
        in_specs=(P("tm", "rows", None, None), P(), P(), P(), P(), P(), P()),
        out_specs=P("tm", "rows", None, None),
        check_vma=False,
    )
```
